32 devices in a mesh: wall: 8 (over z, y), span: 4 (over x, core).
Axes of the slice: x: 2, y: 2, z: 4, core: 2. Of those that a mesh axis runs over, the one named last changes fastest.
Arguments:
- random_planes: float32 [8, 3, 128, 4096], P(None, None, 'wall', 'span'), may hold values from -6 to 6
- previous: float32 [3, 128, 4096], P(None, 'wall', 'span'), may hold values from -6 to 6
- half_width: int32 [128], P('wall'), may hold values from 1 to 32
- time_scale: float32 [3, 128], P(None, 'wall'), may hold values from 1 to 16
- lund_factor: float32 [6, 128], P(None, 'wall'), may hold values from -4 to 4
- mean_velocity: float32 [128], P('wall'), may hold values from 0.5 to 1.5
Outputs:
- velocity: float32 [8, 3, 128, 4096], P(None, None, 'wall', 'span')
- filter_state: float32 [3, 128, 4096], P(None, 'wall', 'span')
The draws below stay inside these ranges and needn't reach their ends.
All inputs are finite; a program needn't handle non-finite values.
Results may differ from the reference program's by a relative error of at most 0.000064.
Values sent between devices are 32-bit elements; how exact they have to be, the bound alone decides.
A program may use at most 128 MiB of HBM per device.

```python
import math
import jax
import jax.numpy as jnp
from jax import lax

STEPS = 8
HMAX = 32
HZ = 24
NY = 128
NZ = 4096


def set_ends(values, own_key, smallest, largest):
    index_at = [jax.random.randint(jax.random.fold_in(own_key, axis), (), 0, length) for axis, length in enumerate(values.shape)]
    longest = values.shape.index(max(values.shape))
    beside = index_at[:longest] + [(index_at[longest] + 1) % values.shape[longest]] + index_at[longest + 1:]
    return values.at[tuple(index_at)].set(smallest).at[tuple(beside)].set(largest)


def steps_of(rng, dims, split, low, largest):
    loudness, own = 1.0, jax.random.fold_in(rng, 6)
    for position, blocks in split:
        heights = jnp.exp(jax.random.uniform(jax.random.fold_in(own, position), (blocks,), jnp.float32, low / len(split), largest / len(split)))
        loudness = loudness * jnp.repeat(heights, dims[position] // blocks).reshape([-1 if axis == position else 1 for axis in range(len(dims))])
    return loudness


def centred(stream_key, extent, scale, most, pieces=(), kind=jnp.bfloat16):
    array = jax.random.normal(stream_key, extent, jnp.float32) * scale
    if len(pieces) > 0:
        array = steps_of(stream_key, extent, pieces, -0.22, 0.18) * array
    return jnp.clip(array, min=-most, max=most).astype(kind)


def setup_inputs(seed: int = 0) -> dict:
    keys = jax.random.split(jax.random.key(seed), 7)
    return {
        "random_planes": centred(keys[0], (STEPS, 3, NY, NZ), 1.0, 6.0, ((2, 8), (3, 4)), jnp.float32),
        "previous": centred(keys[1], (3, NY, NZ), 1.0, 6.0, ((1, 8), (2, 4)), jnp.float32),
        "half_width": set_ends(jax.random.randint(keys[2], (NY,), 1, HMAX + 1), jax.random.fold_in(keys[2], 1), 1, HMAX).astype(jnp.int32),
        "time_scale": jnp.clip(jnp.exp(math.log(16.0) - 2.7725887 * jax.random.uniform(keys[3], (3, NY), jnp.float32) ** steps_of(keys[3], (3, NY), ((1, 8),), -0.2, 0.2)), 1.0, 16.0),
        "lund_factor": centred(keys[4], (6, NY), 1.0, 4.0, ((1, 8),), jnp.float32),
        "mean_velocity": jnp.clip(0.5 + 1.0 * jax.random.uniform(keys[5], (NY,), jnp.float32) ** steps_of(keys[5], (NY,), ((0, 8),), -0.2, 0.2), 0.5, 1.5),
    }


def unit_weights(widths, reach):
    offsets = jnp.arange(-reach, reach + 1, dtype=jnp.int32)
    spread = widths.astype(jnp.float32)[:, None]
    distance = offsets.astype(jnp.float32)[None, :]
    shaped = jnp.where(jnp.abs(offsets)[None, :] <= widths[:, None], jnp.exp(-2.0 * math.pi * distance * distance / (spread * spread)), 0.0)
    return shaped / jnp.sqrt(lax.optimization_barrier(jnp.sum(shaped * shaped, axis=1, keepdims=True)))

def reference(random_planes, previous, half_width, time_scale, lund_factor, mean_velocity):
    wall_weights = unit_weights(half_width, HMAX)
    span_weights = unit_weights(jnp.full((1,), HZ, jnp.int32), HZ)[0]
    retain = jnp.exp(-math.pi / (2.0 * time_scale))[:, :, None]
    inject = jnp.sqrt(1.0 - jnp.exp(-math.pi / time_scale))[:, :, None]
    factor = lund_factor[:, :, None]

    def one_step(current, plane):
        padded = jnp.pad(plane, ((0, 0), (HMAX, HMAX), (0, 0)))

        def add_wall(offset, total):
            start = offset.astype(jnp.int32)
            rows = lax.dynamic_slice_in_dim(padded, start, NY, 1)
            weight = lax.dynamic_slice_in_dim(wall_weights, start, 1, 1)
            return total + weight[None, :, :] * rows
        wall_pass = lax.fori_loop(0, 2 * HMAX + 1, add_wall, jnp.zeros_like(plane))
        wrapped = jnp.concatenate([wall_pass[:, :, NZ - HZ:], wall_pass, wall_pass[:, :, :HZ]], axis=2)

        def add_span(offset, total):
            start = offset.astype(jnp.int32)
            cells = lax.dynamic_slice_in_dim(wrapped, start, NZ, 2)
            weight = lax.dynamic_index_in_dim(span_weights, start, 0, keepdims=False)
            return total + weight * cells
        filtered = lax.fori_loop(0, 2 * HZ + 1, add_span, jnp.zeros_like(plane))
        current = retain * current + inject * filtered
        stream = mean_velocity[:, None] + factor[0] * current[0]
        normal = factor[1] * current[0] + factor[2] * current[1]
        spanwise = factor[3] * current[0] + factor[4] * current[1] + factor[5] * current[2]
        return (current, jnp.stack([stream, normal, spanwise]))
    final, velocities = lax.scan(one_step, previous, random_planes)
    return (velocities, final)
```

```python
import functools
import math

import jax
import jax.numpy as jnp
from jax import lax
from jax.experimental import pallas as pl
from jax.experimental.pallas import tpu as pltpu
from jax.sharding import PartitionSpec as P

HMAX = 32
HZ = 24
LANES = 128
MESH = pl.DeviceIdType.MESH
BF16 = jnp.bfloat16
F32 = jnp.float32

GATHER, UP_OWN, UP_FWD, DOWN_OWN, DOWN_FWD, RETURN, HALO_LEFT, HALO_RIGHT = range(8)
KINDS = 8


def halves(x):
    head = x.astype(BF16)
    return head, (x - head.astype(F32)).astype(BF16)


def columns_of(row):
    n = row.shape[1]
    diagonal = lax.broadcasted_iota(jnp.int32, (n, n), 0) == lax.broadcasted_iota(jnp.int32, (n, n), 1)
    return jnp.sum(jnp.where(diagonal, jnp.broadcast_to(row, (n, n)), 0.0), axis=1, keepdims=True)


def kernel(
    planes, previous, width, scale, lund, mean, velocity, state,
    ext, share, full, out, field, other_width, wall_w, span_head, span_rest,
    send, recv, local, drain, width_sem,
):
    steps, parts, rows, cells = planes.shape
    half = cells // 2
    pair_rows = 2 * rows
    reach = HMAX
    pairs = lax.axis_size("wall") // 2
    spans = lax.axis_size("span")
    wall = lax.axis_index("wall")
    span = lax.axis_index("span")
    pair = wall // 2
    side = wall % 2
    partner = wall + 1 - 2 * side
    right = (span + 1) % spans
    left = (span + spans - 1) % spans
    has_lower = pair > 0
    has_upper = pair < pairs - 1

    barrier = pltpu.get_barrier_semaphore()

    def greet(wall_at, span_at):
        pl.semaphore_signal(
            barrier, inc=1, device_id={"wall": wall_at, "span": span_at}, device_id_type=MESH
        )

    greet(partner, span)
    for beside in (left, right):
        greet(wall, beside)
        greet(partner, beside)

    @pl.when(has_lower)
    def _():
        greet(wall - 2, span)

    @pl.when(has_upper)
    def _():
        greet(wall + 2, span)

    own_rows = pl.ds(pl.multiple_of(rows * side, rows), rows)
    other_rows = pl.ds(pl.multiple_of(rows * (1 - side), rows), rows)
    own_mid = pl.ds(pl.multiple_of(reach + rows * side, rows), rows)
    other_mid = pl.ds(pl.multiple_of(reach + rows * (1 - side), rows), rows)
    own_top = pl.ds(pl.multiple_of(reach + pair_rows + rows * side, rows), rows)
    other_top = pl.ds(pl.multiple_of(reach + pair_rows + rows * (1 - side), rows), rows)
    own_half = pl.ds(pl.multiple_of(half * side, LANES), half)
    other_half = pl.ds(pl.multiple_of(half * (1 - side), LANES), half)
    own_cells = pl.ds(pl.multiple_of(LANES + half * side, LANES), half)
    other_cells = pl.ds(pl.multiple_of(LANES + half * (1 - side), LANES), half)
    edge_in_half = pl.ds(pl.multiple_of((half - LANES) * side, LANES), LANES)
    edge_in_full = pl.ds(pl.multiple_of(LANES + (cells - LANES) * side, LANES), LANES)
    halo_there = pl.ds(pl.multiple_of((LANES + cells) * (1 - side), LANES), LANES)
    toward = (span + spans + 2 * side - 1) % spans
    halo_kind = HALO_LEFT + 1 - side

    def remote(source, target, send_at, recv_at, wall_at, span_at):
        return pltpu.make_async_remote_copy(
            src_ref=source, dst_ref=target, send_sem=send.at[send_at], recv_sem=recv.at[recv_at],
            device_id={"wall": wall_at, "span": span_at}, device_id_type=MESH,
        )

    def gather(s):
        at = GATHER * steps + s
        return remote(planes.at[s, :, :, other_half], ext.at[s, :, own_mid, :], at, at, partner, span)

    def up_own(s):
        at = UP_OWN * steps + s
        return remote(planes.at[s, :, :, own_half], ext.at[s, :, own_rows, :], at, at, wall + 2, span)

    def up_fwd(s):
        at = UP_FWD * steps + s
        return remote(ext.at[s, :, other_mid, :], ext.at[s, :, other_rows, :], at, at, wall + 2, span)

    def down_own(s):
        at = DOWN_OWN * steps + s
        return remote(planes.at[s, :, :, own_half], ext.at[s, :, own_top, :], at, at, wall - 2, span)

    def down_fwd(s):
        at = DOWN_FWD * steps + s
        return remote(ext.at[s, :, other_mid, :], ext.at[s, :, other_top, :], at, at, wall - 2, span)

    def give_back(s):
        at = RETURN * steps + s
        return remote(share.at[s], full.at[s, :, :, own_cells], at, at, partner, span)

    def halo_partner(s):
        return remote(
            share.at[s, :, :, edge_in_half], full.at[s, :, :, halo_there],
            HALO_LEFT * steps + s, halo_kind * steps + s, partner, toward,
        )

    def halo_own(s):
        return remote(
            full.at[s, :, :, edge_in_full], full.at[s, :, :, halo_there],
            HALO_RIGHT * steps + s, halo_kind * steps + s, wall, toward,
        )

    def arrival(target, kind, s):
        at = kind * steps + s
        return remote(target, target, at, at, partner, span)

    own_in = [
        pltpu.make_async_copy(planes.at[s, :, :, own_half], ext.at[s, :, own_mid, :], local.at[s])
        for s in range(steps)
    ]
    field_in = pltpu.make_async_copy(previous, field, local.at[steps])
    width_out = pltpu.make_async_remote_copy(
        src_ref=width, dst_ref=other_width, send_sem=width_sem.at[0], recv_sem=width_sem.at[1],
        device_id={"wall": partner, "span": span}, device_id_type=MESH,
    )

    pl.semaphore_wait(barrier, 5 + has_lower.astype(jnp.int32) + has_upper.astype(jnp.int32))

    width_out.start()
    for s in range(steps):
        gather(s).start()

        @pl.when(has_upper)
        def _():
            up_own(s).start()

        @pl.when(has_lower)
        def _():
            down_own(s).start()

    field_in.start()
    for s in range(steps):
        own_in[s].start()

    @pl.when(pair == 0)
    def _():
        for s in range(steps):
            ext[s, :, 0:reach, :] = jnp.zeros((parts, reach, half), F32)

    @pl.when(pair == pairs - 1)
    def _():
        for s in range(steps):
            ext[s, :, reach + pair_rows:, :] = jnp.zeros((parts, reach, half), F32)

    tile = 2 * LANES
    depth = tile + 2 * LANES
    offset = (
        lax.broadcasted_iota(jnp.int32, (depth, tile), 0)
        - lax.broadcasted_iota(jnp.int32, (depth, tile), 1)
        - LANES
    )
    norm = math.sqrt(sum(math.exp(-2.0 * math.pi * j * j / (HZ * HZ)) ** 2 for j in range(-HZ, HZ + 1)))
    distance = offset.astype(F32)
    band = jnp.where(
        jnp.abs(offset) <= HZ, jnp.exp(distance * distance * (-2.0 * math.pi / (HZ * HZ))), 0.0
    ) * (1.0 / norm)
    head, rest = halves(band)
    span_head[...] = head
    span_rest[...] = rest

    retain_rows = jnp.exp(-math.pi / (2.0 * scale[...]))
    inject_rows = jnp.sqrt(1.0 - jnp.exp(-math.pi / scale[...]))
    retain = [columns_of(retain_rows[c:c + 1]) for c in range(parts)]
    inject = [columns_of(inject_rows[c:c + 1]) for c in range(parts)]
    factor = [columns_of(lund[i:i + 1, :]) for i in range(6)]
    drift = columns_of(mean[...])

    width_out.wait()
    depth_w = reach + pair_rows + reach
    lane = lax.broadcasted_iota(jnp.int32, (rows, 2 * depth_w), 1)
    line = lax.broadcasted_iota(jnp.int32, (rows, 2 * depth_w), 0)
    source = jnp.where(lane >= depth_w, lane - depth_w, lane)

    def wall_weights(widths, first):
        spread = columns_of(widths.astype(F32))
        apart = (source - reach - line - first).astype(F32)
        shaped = jnp.where(
            jnp.abs(apart) <= spread, jnp.exp(-2.0 * math.pi * apart * apart / (spread * spread)), 0.0
        )
        once = jnp.where(lane < depth_w, shaped * shaped, 0.0)
        return shaped / jnp.sqrt(jnp.sum(once, axis=1, keepdims=True))

    weights = jnp.concatenate(
        [wall_weights(width[...], rows * side), wall_weights(other_width[...], rows * (1 - side))], axis=0
    )
    head = weights.astype(BF16).astype(F32)
    first_copy = lax.broadcasted_iota(jnp.int32, weights.shape, 1) < depth_w
    wall_w[...] = jnp.concatenate([head, jnp.where(first_copy, weights - head, 0.0)], axis=0).astype(BF16)

    for s in range(steps):
        arrival(ext.at[s, :, other_mid, :], GATHER, s).wait_recv()

        @pl.when(has_upper)
        def _():
            up_fwd(s).start()

        @pl.when(has_lower)
        def _():
            down_fwd(s).start()

    field_in.wait()
    current = [field[c] for c in range(parts)]

    def finish(s, current):
        arrival(full.at[s, :, :, other_cells], RETURN, s).wait_recv()
        arrival(full.at[s, :, :, 0:LANES], HALO_LEFT, s).wait_recv()
        arrival(full.at[s, :, :, LANES + cells:], HALO_RIGHT, s).wait_recv()
        head, rest = halves(full[s].reshape(parts * rows, cells + 2 * LANES))
        tiles = cells // tile
        heads = jnp.concatenate([head[:, tile * t:tile * t + depth] for t in range(tiles)], axis=0)
        rests = jnp.concatenate([rest[:, tile * t:tile * t + depth] for t in range(tiles)], axis=0)
        count = heads.shape[0]
        both = jnp.dot(jnp.concatenate([heads, rests], axis=0), span_head[...], preferred_element_type=F32)
        low = jnp.dot(heads, span_rest[...], preferred_element_type=F32)
        total = both[:count] + both[count:] + low
        step = parts * rows
        filtered = jnp.concatenate([total[step * t:step * (t + 1)] for t in range(tiles)], axis=1)
        new = [
            retain[c] * current[c] + inject[c] * filtered[rows * c:rows * (c + 1)] for c in range(parts)
        ]
        out[s, 0] = drift + factor[0] * new[0]
        out[s, 1] = factor[1] * new[0] + factor[2] * new[1]
        out[s, 2] = factor[3] * new[0] + factor[4] * new[1] + factor[5] * new[2]
        pltpu.make_async_copy(out.at[s], velocity.at[s], drain.at[s]).start()
        return new

    for s in range(steps):
        own_in[s].wait()

        @pl.when(has_lower)
        def _():
            arrival(ext.at[s, :, own_rows, :], UP_OWN, s).wait_recv()
            arrival(ext.at[s, :, other_rows, :], UP_FWD, s).wait_recv()

        @pl.when(has_upper)
        def _():
            arrival(ext.at[s, :, own_top, :], DOWN_OWN, s).wait_recv()
            arrival(ext.at[s, :, other_top, :], DOWN_FWD, s).wait_recv()

        for c in range(parts):
            head, rest = halves(ext[s, c])
            made = jnp.dot(
                wall_w[...], jnp.concatenate([head, rest], axis=0), preferred_element_type=F32
            )
            passed = made[:pair_rows] + made[pair_rows:]
            share[s, c] = passed[rows:]
            full[s, c, :, own_cells] = passed[:rows]
        give_back(s).start()
        halo_partner(s).start()
        halo_own(s).start()
        if s > 0:
            current = finish(s - 1, current)
    current = finish(steps - 1, current)
    for c in range(parts):
        field[c] = current[c]
    state_out = pltpu.make_async_copy(field, state, drain.at[steps])
    state_out.start()

    for s in range(steps):
        gather(s).wait_send()
        give_back(s).wait_send()
        halo_partner(s).wait_send()
        halo_own(s).wait_send()

        @pl.when(has_upper)
        def _():
            up_own(s).wait_send()
            up_fwd(s).wait_send()

        @pl.when(has_lower)
        def _():
            down_own(s).wait_send()
            down_fwd(s).wait_send()

        pltpu.make_async_copy(out.at[s], velocity.at[s], drain.at[s]).wait()
    state_out.wait()


def shards(random_planes, previous, half_width, time_scale, lund_factor, mean_velocity):
    steps, parts, rows, cells = random_planes.shape
    pair_rows = 2 * rows
    assert pair_rows >= HMAX and lax.axis_size("wall") % 2 == 0
    depth = HMAX + pair_rows + HMAX
    any_space = pl.BlockSpec(memory_space=pl.ANY)
    vmem = pl.BlockSpec(memory_space=pltpu.VMEM)
    dma = pltpu.SemaphoreType.DMA
    return pl.pallas_call(
        kernel,
        out_shape=(
            jax.ShapeDtypeStruct(random_planes.shape, F32),
            jax.ShapeDtypeStruct(previous.shape, F32),
        ),
        in_specs=[any_space, any_space, vmem, vmem, vmem, vmem],
        out_specs=(any_space, any_space),
        scratch_shapes=[
            pltpu.VMEM((steps, parts, depth, cells // 2), F32),
            pltpu.VMEM((steps, parts, rows, cells // 2), F32),
            pltpu.VMEM((steps, parts, rows, cells + 2 * LANES), F32),
            pltpu.VMEM((steps, parts, rows, cells), F32),
            pltpu.VMEM((parts, rows, cells), F32),
            pltpu.VMEM((1, rows), jnp.int32),
            pltpu.VMEM((2 * pair_rows, 2 * depth), BF16),
            pltpu.VMEM((4 * LANES, 2 * LANES), BF16),
            pltpu.VMEM((4 * LANES, 2 * LANES), BF16),
            dma((KINDS * steps,)),
            dma((KINDS * steps,)),
            dma((steps + 1,)),
            dma((steps + 1,)),
            dma((2,)),
        ],
        compiler_params=pltpu.CompilerParams(collective_id=0, has_side_effects=True),
        name="inflow",
    )(
        random_planes, previous, half_width.reshape(1, rows), time_scale, lund_factor,
        mean_velocity.reshape(1, rows),
    )


def solution(mesh):
    in_specs = (
        P(None, None, "wall", "span"),
        P(None, "wall", "span"),
        P("wall"),
        P(None, "wall"),
        P(None, "wall"),
        P("wall"),
    )
    out_specs = (P(None, None, "wall", "span"), P(None, "wall", "span"))
    return jax.shard_map(shards, mesh=mesh, in_specs=in_specs, out_specs=out_specs, check_vma=False)
```

```python
import functools
import math

import jax
import jax.numpy as jnp
from jax import lax
from jax.experimental import pallas as pl
from jax.experimental.pallas import tpu as pltpu
from jax.sharding import PartitionSpec as P

HMAX = 32
HZ = 24
LANES = 128
MESH = pl.DeviceIdType.MESH
BF16 = jnp.bfloat16
F32 = jnp.float32

GATHER, UP_OWN, UP_FWD, DOWN_OWN, DOWN_FWD, RETURN, HALO_LEFT, HALO_RIGHT = range(8)
KINDS = 8
AHEAD = 2
LEAD = 4
VMEM_LIMIT = 24 * 2**20


def halves(x):
    head = x.astype(BF16)
    return head, (x - head.astype(F32)).astype(BF16)


def chunks_of(steps, parts):
    return [(s, 0, parts) for s in range(steps - 1)] + [(steps - 1, c, c + 1) for c in range(parts)]


def columns_of(row):
    n = row.shape[1]
    diagonal = lax.broadcasted_iota(jnp.int32, (n, n), 0) == lax.broadcasted_iota(jnp.int32, (n, n), 1)
    return jnp.sum(jnp.where(diagonal, jnp.broadcast_to(row, (n, n)), 0.0), axis=1, keepdims=True)


def kernel(
    planes, previous, width, scale, lund, mean, velocity, state,
    ext, share, full, field, other_width, wall_w, span_head, span_rest,
    send, recv, local, width_sem,
):
    steps, parts, rows, cells = planes.shape
    chunks = chunks_of(steps, parts)
    count = len(chunks)
    half = cells // 2
    pair_rows = 2 * rows
    reach = HMAX
    pairs = lax.axis_size("wall") // 2
    spans = lax.axis_size("span")
    wall = lax.axis_index("wall")
    span = lax.axis_index("span")
    pair = wall // 2
    side = wall % 2
    partner = wall + 1 - 2 * side
    right = (span + 1) % spans
    left = (span + spans - 1) % spans
    has_lower = pair > 0
    has_upper = pair < pairs - 1

    barrier = pltpu.get_barrier_semaphore()

    def greet(wall_at, span_at):
        pl.semaphore_signal(
            barrier, inc=1, device_id={"wall": wall_at, "span": span_at}, device_id_type=MESH
        )

    greet(partner, span)
    for beside in (left, right):
        greet(wall, beside)
        greet(partner, beside)

    @pl.when(has_lower)
    def _():
        greet(wall - 2, span)

    @pl.when(has_upper)
    def _():
        greet(wall + 2, span)

    own_rows = pl.ds(pl.multiple_of(rows * side, rows), rows)
    other_rows = pl.ds(pl.multiple_of(rows * (1 - side), rows), rows)
    own_mid = pl.ds(pl.multiple_of(reach + rows * side, rows), rows)
    other_mid = pl.ds(pl.multiple_of(reach + rows * (1 - side), rows), rows)
    own_top = pl.ds(pl.multiple_of(reach + pair_rows + rows * side, rows), rows)
    other_top = pl.ds(pl.multiple_of(reach + pair_rows + rows * (1 - side), rows), rows)
    own_half = pl.ds(pl.multiple_of(half * side, LANES), half)
    other_half = pl.ds(pl.multiple_of(half * (1 - side), LANES), half)
    own_cells = pl.ds(pl.multiple_of(LANES + half * side, LANES), half)
    other_cells = pl.ds(pl.multiple_of(LANES + half * (1 - side), LANES), half)
    edge_in_half = pl.ds(pl.multiple_of((half - LANES) * side, LANES), LANES)
    edge_in_full = pl.ds(pl.multiple_of(LANES + (cells - LANES) * side, LANES), LANES)
    halo_there = pl.ds(pl.multiple_of((LANES + cells) * (1 - side), LANES), LANES)
    other_edge_in_full = pl.ds(pl.multiple_of(LANES + (cells - LANES) * (1 - side), LANES), LANES)
    other_halo_there = pl.ds(pl.multiple_of((LANES + cells) * side, LANES), LANES)
    toward = (span + spans + 2 * side - 1) % spans
    away = (span + spans + 1 - 2 * side) % spans

    def parts_of(k):
        s, first, end = chunks[k]
        return s, pl.ds(first, end - first)

    def remote(source, target, send_at, recv_at, wall_at, span_at):
        return pltpu.make_async_remote_copy(
            src_ref=source, dst_ref=target, send_sem=send.at[send_at], recv_sem=recv.at[recv_at],
            device_id={"wall": wall_at, "span": span_at}, device_id_type=MESH,
        )

    def gather(k):
        at = GATHER * count + k
        s, c = parts_of(k)
        return remote(planes.at[s, c, :, other_half], ext.at[s, c, own_mid, :], at, at, partner, span)

    def up_own(k):
        at = UP_OWN * count + k
        s, c = parts_of(k)
        return remote(planes.at[s, c, :, own_half], ext.at[s, c, own_rows, :], at, at, wall + 2, span)

    def up_fwd(k):
        at = UP_FWD * count + k
        s, c = parts_of(k)
        return remote(ext.at[s, c, other_mid, :], ext.at[s, c, other_rows, :], at, at, wall + 2, span)

    def down_own(k):
        at = DOWN_OWN * count + k
        s, c = parts_of(k)
        return remote(planes.at[s, c, :, own_half], ext.at[s, c, own_top, :], at, at, wall - 2, span)

    def down_fwd(k):
        at = DOWN_FWD * count + k
        s, c = parts_of(k)
        return remote(ext.at[s, c, other_mid, :], ext.at[s, c, other_top, :], at, at, wall - 2, span)

    def give_back(k):
        at = RETURN * count + k
        s, c = parts_of(k)
        return remote(share.at[s, c], full.at[s, c, :, own_cells], at, at, partner, span)

    def own_edge(k):
        s, c = parts_of(k)
        return remote(
            full.at[s, c, :, edge_in_full], full.at[s, c, :, halo_there],
            HALO_LEFT * count + k, (HALO_LEFT + 1 - side) * count + k, wall, toward,
        )

    def other_edge(k):
        s, c = parts_of(k)
        if s < steps - 1:
            return remote(
                full.at[s, c, :, other_edge_in_full], full.at[s, c, :, other_halo_there],
                HALO_RIGHT * count + k, (HALO_LEFT + side) * count + k, wall, away,
            )
        return remote(
            share.at[s, c, :, edge_in_half], full.at[s, c, :, halo_there],
            HALO_RIGHT * count + k, (HALO_LEFT + 1 - side) * count + k, partner, toward,
        )

    def arrival(kind, k, row_at, cell_at, buffer):
        at = kind * count + k
        s, c = parts_of(k)
        target = buffer.at[s, c, row_at, cell_at]
        return remote(target, target, at, at, partner, span)

    own_in = [
        pltpu.make_async_copy(planes.at[s, :, :, own_half], ext.at[s, :, own_mid, :], local.at[s])
        for s in range(steps)
    ]
    field_in = pltpu.make_async_copy(previous, field, local.at[steps])
    width_out = pltpu.make_async_remote_copy(
        src_ref=width, dst_ref=other_width, send_sem=width_sem.at[0], recv_sem=width_sem.at[1],
        device_id={"wall": partner, "span": span}, device_id_type=MESH,
    )

    pl.semaphore_wait(barrier, 5 + has_lower.astype(jnp.int32) + has_upper.astype(jnp.int32))

    width_out.start()
    def own_out(k):
        @pl.when(has_upper)
        def _():
            up_own(k).start()

        @pl.when(has_lower)
        def _():
            down_own(k).start()

    for k in range(AHEAD):
        gather(k).start()
        own_out(k)
    for k in range(AHEAD, count):
        gather(k).start()

    field_in.start()
    for s in range(steps):
        own_in[s].start()

    @pl.when(pair == 0)
    def _():
        for s in range(steps):
            ext[s, :, 0:reach, :] = jnp.zeros((parts, reach, half), F32)

    @pl.when(pair == pairs - 1)
    def _():
        for s in range(steps):
            ext[s, :, reach + pair_rows:, :] = jnp.zeros((parts, reach, half), F32)

    tile = 2 * LANES
    depth = tile + 2 * LANES
    offset = (
        lax.broadcasted_iota(jnp.int32, (depth, tile), 0)
        - lax.broadcasted_iota(jnp.int32, (depth, tile), 1)
        - LANES
    )
    norm = math.sqrt(sum(math.exp(-2.0 * math.pi * j * j / (HZ * HZ)) ** 2 for j in range(-HZ, HZ + 1)))
    distance = offset.astype(F32)
    band = jnp.where(
        jnp.abs(offset) <= HZ, jnp.exp(distance * distance * (-2.0 * math.pi / (HZ * HZ))), 0.0
    ) * (1.0 / norm)
    head, rest = halves(band)
    span_head[...] = head
    span_rest[...] = rest

    retain_rows = jnp.exp(-math.pi / (2.0 * scale[...]))
    inject_rows = jnp.sqrt(1.0 - jnp.exp(-math.pi / scale[...]))
    retain = [columns_of(retain_rows[c:c + 1]) for c in range(parts)]
    inject = [columns_of(inject_rows[c:c + 1]) for c in range(parts)]
    factor = [columns_of(lund[i:i + 1, :]) for i in range(6)]
    drift = columns_of(mean[...])

    width_out.wait()
    depth_w = reach + pair_rows + reach
    lane = lax.broadcasted_iota(jnp.int32, (rows, 2 * depth_w), 1)
    line = lax.broadcasted_iota(jnp.int32, (rows, 2 * depth_w), 0)
    source = jnp.where(lane >= depth_w, lane - depth_w, lane)

    def wall_weights(widths, first):
        spread = columns_of(widths.astype(F32))
        apart = (source - reach - line - first).astype(F32)
        shaped = jnp.where(
            jnp.abs(apart) <= spread, jnp.exp(-2.0 * math.pi * apart * apart / (spread * spread)), 0.0
        )
        once = jnp.where(lane < depth_w, shaped * shaped, 0.0)
        return shaped / jnp.sqrt(jnp.sum(once, axis=1, keepdims=True))

    weights = jnp.concatenate(
        [wall_weights(width[...], rows * side), wall_weights(other_width[...], rows * (1 - side))], axis=0
    )
    head = weights.astype(BF16).astype(F32)
    first_copy = lax.broadcasted_iota(jnp.int32, weights.shape, 1) < depth_w
    wall_w[...] = jnp.concatenate([head, jnp.where(first_copy, weights - head, 0.0)], axis=0).astype(BF16)

    def forward(k):
        arrival(GATHER, k, other_mid, slice(None), ext).wait_recv()

        @pl.when(has_upper)
        def _():
            up_fwd(k).start()

        @pl.when(has_lower)
        def _():
            down_fwd(k).start()

        if k + AHEAD < count:
            own_out(k + AHEAD)

    def wall_pass(k):
        s, first, end = chunks[k]
        if first == 0:
            own_in[s].wait()

        @pl.when(has_lower)
        def _():
            arrival(UP_OWN, k, own_rows, slice(None), ext).wait_recv()
            arrival(UP_FWD, k, other_rows, slice(None), ext).wait_recv()

        @pl.when(has_upper)
        def _():
            arrival(DOWN_OWN, k, own_top, slice(None), ext).wait_recv()
            arrival(DOWN_FWD, k, other_top, slice(None), ext).wait_recv()

        for c in range(first, end):
            head, rest = halves(ext[s, c])
            made = jnp.dot(
                wall_w[...], jnp.concatenate([head, rest], axis=0), preferred_element_type=F32
            )
            passed = made[:pair_rows] + made[pair_rows:]
            share[s, c] = passed[rows:]
            full[s, c, :, own_cells] = passed[:rows]
        give_back(k).start()
        own_edge(k).start()
        if s == steps - 1:
            other_edge(k).start()

    def take_back(k):
        arrival(RETURN, k, slice(None), other_cells, full).wait_recv()
        if chunks[k][0] < steps - 1:
            other_edge(k).start()

    field_in.wait()
    current = [field[c] for c in range(parts)]

    def finish(s, current):
        for k in range(count):
            if chunks[k][0] == s:
                arrival(HALO_LEFT, k, slice(None), slice(0, LANES), full).wait_recv()
                arrival(HALO_RIGHT, k, slice(None), slice(LANES + cells, None), full).wait_recv()
        head, rest = halves(full[s].reshape(parts * rows, cells + 2 * LANES))
        tiles = cells // tile
        heads = jnp.concatenate([head[:, tile * t:tile * t + depth] for t in range(tiles)], axis=0)
        rests = jnp.concatenate([rest[:, tile * t:tile * t + depth] for t in range(tiles)], axis=0)
        height = heads.shape[0]
        both = jnp.dot(jnp.concatenate([heads, rests], axis=0), span_head[...], preferred_element_type=F32)
        low = jnp.dot(heads, span_rest[...], preferred_element_type=F32)
        total = both[:height] + both[height:] + low
        step = parts * rows
        filtered = jnp.concatenate([total[step * t:step * (t + 1)] for t in range(tiles)], axis=1)
        new = [
            retain[c] * current[c] + inject[c] * filtered[rows * c:rows * (c + 1)] for c in range(parts)
        ]
        velocity[s, 0] = drift + factor[0] * new[0]
        velocity[s, 1] = factor[1] * new[0] + factor[2] * new[1]
        velocity[s, 2] = factor[3] * new[0] + factor[4] * new[1] + factor[5] * new[2]
        return new

    forwarded = taken = finished = 0
    for k in range(count):
        while forwarded < min(count, LEAD + 2 * k):
            forward(forwarded)
            forwarded += 1
        wall_pass(k)
        if k > 2:
            while taken < k - 1:
                take_back(taken)
                taken += 1
            while finished < min(steps - 1, k - 2):
                current = finish(finished, current)
                finished += 1
    while taken < count:
        take_back(taken)
        taken += 1
    while finished < steps:
        current = finish(finished, current)
        finished += 1
    for c in range(parts):
        state[c] = current[c]

    for k in range(count):
        gather(k).wait_send()
        give_back(k).wait_send()
        own_edge(k).wait_send()
        other_edge(k).wait_send()

        @pl.when(has_upper)
        def _():
            up_own(k).wait_send()
            up_fwd(k).wait_send()

        @pl.when(has_lower)
        def _():
            down_own(k).wait_send()
            down_fwd(k).wait_send()


def shards(random_planes, previous, half_width, time_scale, lund_factor, mean_velocity):
    steps, parts, rows, cells = random_planes.shape
    pair_rows = 2 * rows
    assert pair_rows >= HMAX and lax.axis_size("wall") % 2 == 0
    depth = HMAX + pair_rows + HMAX
    count = len(chunks_of(steps, parts))
    hbm = pl.BlockSpec(memory_space=pltpu.HBM)
    vmem = pl.BlockSpec(memory_space=pltpu.VMEM)
    dma = pltpu.SemaphoreType.DMA
    return pl.pallas_call(
        kernel,
        out_shape=(
            jax.ShapeDtypeStruct(random_planes.shape, F32),
            jax.ShapeDtypeStruct(previous.shape, F32),
        ),
        in_specs=[hbm, hbm, vmem, vmem, vmem, vmem],
        out_specs=(vmem, vmem),
        scratch_shapes=[
            pltpu.VMEM((steps, parts, depth, cells // 2), F32),
            pltpu.VMEM((steps, parts, rows, cells // 2), F32),
            pltpu.VMEM((steps, parts, rows, cells + 2 * LANES), F32),
            pltpu.VMEM((parts, rows, cells), F32),
            pltpu.VMEM((1, rows), jnp.int32),
            pltpu.VMEM((2 * pair_rows, 2 * depth), BF16),
            pltpu.VMEM((4 * LANES, 2 * LANES), BF16),
            pltpu.VMEM((4 * LANES, 2 * LANES), BF16),
            dma((KINDS * count,)),
            dma((KINDS * count,)),
            dma((steps + 1,)),
            dma((2,)),
        ],
        compiler_params=pltpu.CompilerParams(collective_id=0, has_side_effects=True, vmem_limit_bytes=VMEM_LIMIT),
        name="inflow",
    )(*(
        pltpu.with_memory_space_constraint(array, pltpu.HBM)
        for array in (
            random_planes, previous, half_width.reshape(1, rows), time_scale, lund_factor,
            mean_velocity.reshape(1, rows),
        )
    ))


def solution(mesh):
    in_specs = (
        P(None, None, "wall", "span"),
        P(None, "wall", "span"),
        P("wall"),
        P(None, "wall"),
        P(None, "wall"),
        P("wall"),
    )
    out_specs = (P(None, None, "wall", "span"), P(None, "wall", "span"))
    return jax.shard_map(shards, mesh=mesh, in_specs=in_specs, out_specs=out_specs, check_vma=False)
```

```python
import functools
import math

import jax
import jax.numpy as jnp
from jax import lax
from jax.experimental import pallas as pl
from jax.experimental.pallas import tpu as pltpu
from jax.sharding import PartitionSpec as P

HMAX = 32
HZ = 24
LANES = 128
MESH = pl.DeviceIdType.MESH
BF16 = jnp.bfloat16
F32 = jnp.float32

GATHER, UP_OWN, UP_FWD, DOWN_OWN, DOWN_FWD, RETURN, HALO_LEFT, HALO_RIGHT = range(8)
KINDS = 8
AHEAD = 2
LEAD = 4
VMEM_LIMIT = 24 * 2**20


def halves(x):
    head = x.astype(BF16)
    return head, (x - head.astype(F32)).astype(BF16)


def chunks_of(steps, parts):
    return [(s, 0, parts) for s in range(steps - 1)] + [(steps - 1, c, c + 1) for c in range(parts)]


def columns_of(row):
    n = row.shape[1]
    diagonal = lax.broadcasted_iota(jnp.int32, (n, n), 0) == lax.broadcasted_iota(jnp.int32, (n, n), 1)
    return jnp.sum(jnp.where(diagonal, jnp.broadcast_to(row, (n, n)), 0.0), axis=1, keepdims=True)


def kernel(
    planes, previous, width_hbm, scale_hbm, lund_hbm, mean_hbm, velocity, state,
    ext, share, full, field, width, scale, lund, mean, other_width, wall_w, span_head, span_rest,
    send, recv, local, small, width_sem,
):
    steps, parts, rows, cells = planes.shape
    chunks = chunks_of(steps, parts)
    count = len(chunks)
    half = cells // 2
    pair_rows = 2 * rows
    reach = HMAX
    pairs = lax.axis_size("wall") // 2
    spans = lax.axis_size("span")
    wall = lax.axis_index("wall")
    span = lax.axis_index("span")
    pair = wall // 2
    side = wall % 2
    partner = wall + 1 - 2 * side
    right = (span + 1) % spans
    left = (span + spans - 1) % spans
    has_lower = pair > 0
    has_upper = pair < pairs - 1

    barrier = pltpu.get_barrier_semaphore()

    def greet(wall_at, span_at):
        pl.semaphore_signal(
            barrier, inc=1, device_id={"wall": wall_at, "span": span_at}, device_id_type=MESH
        )

    greet(partner, span)
    for beside in (left, right):
        greet(wall, beside)
        greet(partner, beside)

    @pl.when(has_lower)
    def _():
        greet(wall - 2, span)

    @pl.when(has_upper)
    def _():
        greet(wall + 2, span)

    own_rows = pl.ds(pl.multiple_of(rows * side, rows), rows)
    other_rows = pl.ds(pl.multiple_of(rows * (1 - side), rows), rows)
    own_mid = pl.ds(pl.multiple_of(reach + rows * side, rows), rows)
    other_mid = pl.ds(pl.multiple_of(reach + rows * (1 - side), rows), rows)
    own_top = pl.ds(pl.multiple_of(reach + pair_rows + rows * side, rows), rows)
    other_top = pl.ds(pl.multiple_of(reach + pair_rows + rows * (1 - side), rows), rows)
    own_half = pl.ds(pl.multiple_of(half * side, LANES), half)
    other_half = pl.ds(pl.multiple_of(half * (1 - side), LANES), half)
    own_cells = pl.ds(pl.multiple_of(LANES + half * side, LANES), half)
    other_cells = pl.ds(pl.multiple_of(LANES + half * (1 - side), LANES), half)
    edge_in_half = pl.ds(pl.multiple_of((half - LANES) * side, LANES), LANES)
    edge_in_full = pl.ds(pl.multiple_of(LANES + (cells - LANES) * side, LANES), LANES)
    halo_there = pl.ds(pl.multiple_of((LANES + cells) * (1 - side), LANES), LANES)
    other_edge_in_full = pl.ds(pl.multiple_of(LANES + (cells - LANES) * (1 - side), LANES), LANES)
    other_halo_there = pl.ds(pl.multiple_of((LANES + cells) * side, LANES), LANES)
    toward = (span + spans + 2 * side - 1) % spans
    away = (span + spans + 1 - 2 * side) % spans

    def parts_of(k):
        s, first, end = chunks[k]
        return s, pl.ds(first, end - first)

    def remote(source, target, send_at, recv_at, wall_at, span_at):
        return pltpu.make_async_remote_copy(
            src_ref=source, dst_ref=target, send_sem=send.at[send_at], recv_sem=recv.at[recv_at],
            device_id={"wall": wall_at, "span": span_at}, device_id_type=MESH,
        )

    def gather(k):
        at = GATHER * count + k
        s, c = parts_of(k)
        return remote(planes.at[s, c, :, other_half], ext.at[s, c, own_mid, :], at, at, partner, span)

    def up_own(k):
        at = UP_OWN * count + k
        s, c = parts_of(k)
        return remote(planes.at[s, c, :, own_half], ext.at[s, c, own_rows, :], at, at, wall + 2, span)

    def up_fwd(k):
        at = UP_FWD * count + k
        s, c = parts_of(k)
        return remote(ext.at[s, c, other_mid, :], ext.at[s, c, other_rows, :], at, at, wall + 2, span)

    def down_own(k):
        at = DOWN_OWN * count + k
        s, c = parts_of(k)
        return remote(planes.at[s, c, :, own_half], ext.at[s, c, own_top, :], at, at, wall - 2, span)

    def down_fwd(k):
        at = DOWN_FWD * count + k
        s, c = parts_of(k)
        return remote(ext.at[s, c, other_mid, :], ext.at[s, c, other_top, :], at, at, wall - 2, span)

    def give_back(k):
        at = RETURN * count + k
        s, c = parts_of(k)
        return remote(share.at[s, c], full.at[s, c, :, own_cells], at, at, partner, span)

    def own_edge(k):
        s, c = parts_of(k)
        return remote(
            full.at[s, c, :, edge_in_full], full.at[s, c, :, halo_there],
            HALO_LEFT * count + k, (HALO_LEFT + 1 - side) * count + k, wall, toward,
        )

    def other_edge(k):
        s, c = parts_of(k)
        if s < steps - 1:
            return remote(
                full.at[s, c, :, other_edge_in_full], full.at[s, c, :, other_halo_there],
                HALO_RIGHT * count + k, (HALO_LEFT + side) * count + k, wall, away,
            )
        return remote(
            share.at[s, c, :, edge_in_half], full.at[s, c, :, halo_there],
            HALO_RIGHT * count + k, (HALO_LEFT + 1 - side) * count + k, partner, toward,
        )

    def arrival(kind, k, row_at, cell_at, buffer):
        at = kind * count + k
        s, c = parts_of(k)
        target = buffer.at[s, c, row_at, cell_at]
        return remote(target, target, at, at, partner, span)

    own_in = [
        pltpu.make_async_copy(planes.at[s, :, :, own_half], ext.at[s, :, own_mid, :], local.at[s])
        for s in range(steps)
    ]
    field_in = pltpu.make_async_copy(previous, field, local.at[steps])
    small_in = [
        pltpu.make_async_copy(source, target, small.at[i])
        for i, (source, target) in enumerate(
            ((width_hbm, width), (scale_hbm, scale), (lund_hbm, lund), (mean_hbm, mean))
        )
    ]
    width_out = pltpu.make_async_remote_copy(
        src_ref=width_hbm, dst_ref=other_width, send_sem=width_sem.at[0], recv_sem=width_sem.at[1],
        device_id={"wall": partner, "span": span}, device_id_type=MESH,
    )

    pl.semaphore_wait(barrier, 5 + has_lower.astype(jnp.int32) + has_upper.astype(jnp.int32))

    width_out.start()
    def own_out(k):
        @pl.when(has_upper)
        def _():
            up_own(k).start()

        @pl.when(has_lower)
        def _():
            down_own(k).start()

    for k in range(AHEAD):
        gather(k).start()
        own_out(k)
    for k in range(AHEAD, count):
        gather(k).start()

    for copy in small_in:
        copy.start()
    field_in.start()
    for s in range(steps):
        own_in[s].start()

    @pl.when(pair == 0)
    def _():
        for s in range(steps):
            ext[s, :, 0:reach, :] = jnp.zeros((parts, reach, half), F32)

    @pl.when(pair == pairs - 1)
    def _():
        for s in range(steps):
            ext[s, :, reach + pair_rows:, :] = jnp.zeros((parts, reach, half), F32)

    tile = 2 * LANES
    depth = tile + 2 * LANES
    offset = (
        lax.broadcasted_iota(jnp.int32, (depth, tile), 0)
        - lax.broadcasted_iota(jnp.int32, (depth, tile), 1)
        - LANES
    )
    norm = math.sqrt(sum(math.exp(-2.0 * math.pi * j * j / (HZ * HZ)) ** 2 for j in range(-HZ, HZ + 1)))
    distance = offset.astype(F32)
    band = jnp.where(
        jnp.abs(offset) <= HZ, jnp.exp(distance * distance * (-2.0 * math.pi / (HZ * HZ))), 0.0
    ) * (1.0 / norm)
    head, rest = halves(band)
    span_head[...] = head
    span_rest[...] = rest

    for copy in small_in:
        copy.wait()
    retain_rows = jnp.exp(-math.pi / (2.0 * scale[...]))
    inject_rows = jnp.sqrt(1.0 - jnp.exp(-math.pi / scale[...]))
    retain = [columns_of(retain_rows[c:c + 1]) for c in range(parts)]
    inject = [columns_of(inject_rows[c:c + 1]) for c in range(parts)]
    factor = [columns_of(lund[i:i + 1, :]) for i in range(6)]
    drift = columns_of(mean[...])

    width_out.wait()
    depth_w = reach + pair_rows + reach
    lane = lax.broadcasted_iota(jnp.int32, (rows, 2 * depth_w), 1)
    line = lax.broadcasted_iota(jnp.int32, (rows, 2 * depth_w), 0)
    source = jnp.where(lane >= depth_w, lane - depth_w, lane)

    def wall_weights(widths, first):
        spread = columns_of(widths.astype(F32))
        apart = (source - reach - line - first).astype(F32)
        shaped = jnp.where(
            jnp.abs(apart) <= spread, jnp.exp(-2.0 * math.pi * apart * apart / (spread * spread)), 0.0
        )
        once = jnp.where(lane < depth_w, shaped * shaped, 0.0)
        return shaped / jnp.sqrt(jnp.sum(once, axis=1, keepdims=True))

    weights = jnp.concatenate(
        [wall_weights(width[...], rows * side), wall_weights(other_width[...], rows * (1 - side))], axis=0
    )
    head = weights.astype(BF16).astype(F32)
    first_copy = lax.broadcasted_iota(jnp.int32, weights.shape, 1) < depth_w
    wall_w[...] = jnp.concatenate([head, jnp.where(first_copy, weights - head, 0.0)], axis=0).astype(BF16)

    def forward(k):
        arrival(GATHER, k, other_mid, slice(None), ext).wait_recv()

        @pl.when(has_upper)
        def _():
            up_fwd(k).start()

        @pl.when(has_lower)
        def _():
            down_fwd(k).start()

        if k + AHEAD < count:
            own_out(k + AHEAD)

    def wall_pass(k):
        s, first, end = chunks[k]
        if first == 0:
            own_in[s].wait()

        @pl.when(has_lower)
        def _():
            arrival(UP_OWN, k, own_rows, slice(None), ext).wait_recv()
            arrival(UP_FWD, k, other_rows, slice(None), ext).wait_recv()

        @pl.when(has_upper)
        def _():
            arrival(DOWN_OWN, k, own_top, slice(None), ext).wait_recv()
            arrival(DOWN_FWD, k, other_top, slice(None), ext).wait_recv()

        for c in range(first, end):
            head, rest = halves(ext[s, c])
            made = jnp.dot(
                wall_w[...], jnp.concatenate([head, rest], axis=0), preferred_element_type=F32
            )
            passed = made[:pair_rows] + made[pair_rows:]
            share[s, c] = passed[rows:]
            full[s, c, :, own_cells] = passed[:rows]
        give_back(k).start()
        own_edge(k).start()
        if s == steps - 1:
            other_edge(k).start()

    def take_back(k):
        arrival(RETURN, k, slice(None), other_cells, full).wait_recv()
        if chunks[k][0] < steps - 1:
            other_edge(k).start()

    field_in.wait()
    current = [field[c] for c in range(parts)]

    def finish(s, current):
        for k in range(count):
            if chunks[k][0] == s:
                arrival(HALO_LEFT, k, slice(None), slice(0, LANES), full).wait_recv()
                arrival(HALO_RIGHT, k, slice(None), slice(LANES + cells, None), full).wait_recv()
        head, rest = halves(full[s].reshape(parts * rows, cells + 2 * LANES))
        tiles = cells // tile
        heads = jnp.concatenate([head[:, tile * t:tile * t + depth] for t in range(tiles)], axis=0)
        rests = jnp.concatenate([rest[:, tile * t:tile * t + depth] for t in range(tiles)], axis=0)
        height = heads.shape[0]
        both = jnp.dot(jnp.concatenate([heads, rests], axis=0), span_head[...], preferred_element_type=F32)
        low = jnp.dot(heads, span_rest[...], preferred_element_type=F32)
        total = both[:height] + both[height:] + low
        step = parts * rows
        filtered = jnp.concatenate([total[step * t:step * (t + 1)] for t in range(tiles)], axis=1)
        new = [
            retain[c] * current[c] + inject[c] * filtered[rows * c:rows * (c + 1)] for c in range(parts)
        ]
        velocity[s, 0] = drift + factor[0] * new[0]
        velocity[s, 1] = factor[1] * new[0] + factor[2] * new[1]
        velocity[s, 2] = factor[3] * new[0] + factor[4] * new[1] + factor[5] * new[2]
        return new

    forwarded = taken = finished = 0
    for k in range(count):
        while forwarded < min(count, LEAD + 2 * k):
            forward(forwarded)
            forwarded += 1
        wall_pass(k)
        if k > 2:
            while taken < k - 1:
                take_back(taken)
                taken += 1
            while finished < min(steps - 1, k - 2):
                current = finish(finished, current)
                finished += 1
    while taken < count:
        take_back(taken)
        taken += 1
    while finished < steps:
        current = finish(finished, current)
        finished += 1
    for c in range(parts):
        state[c] = current[c]

    for k in range(count):
        gather(k).wait_send()
        give_back(k).wait_send()
        own_edge(k).wait_send()
        other_edge(k).wait_send()

        @pl.when(has_upper)
        def _():
            up_own(k).wait_send()
            up_fwd(k).wait_send()

        @pl.when(has_lower)
        def _():
            down_own(k).wait_send()
            down_fwd(k).wait_send()


def put_out(*refs):
    half = len(refs) // 2
    copies = [
        pltpu.make_async_copy(refs[i], refs[half + i], refs[-1].at[i]) for i in range(2)
    ]
    for copy in copies:
        copy.start()
    for copy in copies:
        copy.wait()


def shards(random_planes, previous, half_width, time_scale, lund_factor, mean_velocity):
    steps, parts, rows, cells = random_planes.shape
    pair_rows = 2 * rows
    assert pair_rows >= HMAX and lax.axis_size("wall") % 2 == 0
    depth = HMAX + pair_rows + HMAX
    count = len(chunks_of(steps, parts))
    hbm = pl.BlockSpec(memory_space=pltpu.HBM)
    vmem = pl.BlockSpec(memory_space=pltpu.VMEM)
    dma = pltpu.SemaphoreType.DMA
    results = pl.pallas_call(
        kernel,
        out_shape=(
            jax.ShapeDtypeStruct(random_planes.shape, F32),
            jax.ShapeDtypeStruct(previous.shape, F32),
        ),
        in_specs=[hbm] * 6,
        out_specs=(vmem, vmem),
        scratch_shapes=[
            pltpu.VMEM((steps, parts, depth, cells // 2), F32),
            pltpu.VMEM((steps, parts, rows, cells // 2), F32),
            pltpu.VMEM((steps, parts, rows, cells + 2 * LANES), F32),
            pltpu.VMEM((parts, rows, cells), F32),
            pltpu.VMEM((1, rows), jnp.int32),
            pltpu.VMEM(time_scale.shape, F32),
            pltpu.VMEM(lund_factor.shape, F32),
            pltpu.VMEM((1, rows), F32),
            pltpu.VMEM((1, rows), jnp.int32),
            pltpu.VMEM((2 * pair_rows, 2 * depth), BF16),
            pltpu.VMEM((4 * LANES, 2 * LANES), BF16),
            pltpu.VMEM((4 * LANES, 2 * LANES), BF16),
            dma((KINDS * count,)),
            dma((KINDS * count,)),
            dma((steps + 1,)),
            dma((4,)),
            dma((2,)),
        ],
        compiler_params=pltpu.CompilerParams(collective_id=0, has_side_effects=True, vmem_limit_bytes=VMEM_LIMIT),
        name="inflow",
    )(*(
        pltpu.with_memory_space_constraint(array, pltpu.HBM)
        for array in (
            random_planes, previous, half_width.reshape(1, rows), time_scale, lund_factor,
            mean_velocity.reshape(1, rows),
        )
    ))
    space = pl.BlockSpec(memory_space=pl.ANY)
    return pl.pallas_call(
        put_out,
        out_shape=tuple(jax.ShapeDtypeStruct(r.shape, r.dtype) for r in results),
        in_specs=[space] * 2,
        out_specs=(hbm, hbm),
        scratch_shapes=[dma((2,))],
        compiler_params=pltpu.CompilerParams(vmem_limit_bytes=VMEM_LIMIT),
        name="put_out",
    )(*results)


def solution(mesh):
    in_specs = (
        P(None, None, "wall", "span"),
        P(None, "wall", "span"),
        P("wall"),
        P(None, "wall"),
        P(None, "wall"),
        P("wall"),
    )
    out_specs = (P(None, None, "wall", "span"), P(None, "wall", "span"))
    return jax.shard_map(shards, mesh=mesh, in_specs=in_specs, out_specs=out_specs, check_vma=False)
```
